32 devices in a mesh: groups: 1, seq: 32 (over z, y, x, core).
Axes of the slice: x: 2, y: 2, z: 4, core: 2. Of those that a mesh axis runs over, the one named last changes fastest.
Arguments:
- queries: bfloat16 [8192, 2048], P(('groups', 'seq')), may hold values from -6 to 6
- keys: bfloat16 [8192, 2048], P(('groups', 'seq')), may hold values from -6 to 6
- values: bfloat16 [8192, 2048], P(('groups', 'seq')), may hold values from -6 to 6
- out_weight: bfloat16 [2048, 2048], replicated, may hold values from -0.125 to 0.125
- out_grad: bfloat16 [8192, 2048], P(('groups', 'seq')), may hold values from -6 to 6
Outputs:
- query_grad: bfloat16 [8192, 2048], P(('groups', 'seq'))
- key_grad: bfloat16 [8192, 2048], P(('groups', 'seq'))
- value_grad: bfloat16 [8192, 2048], P(('groups', 'seq'))
- weight_grad: float32 [2048, 2048], P(('groups', 'seq'))
The draws below stay inside these ranges and needn't reach their ends.
All inputs are finite; a program needn't handle non-finite values.
Results may differ from the reference program's by a relative error of at most 0.0033.
Values sent between devices are 32-bit elements; how exact they have to be, the bound alone decides.
A program may use at most 192 MiB of HBM per device.

```python
import jax
import jax.numpy as jnp
from jax import lax

D = 2048
HEADS = 16
HEAD = 128
TOK_DEV = 256
TOKENS = 8192
HD = 2048


def steps_of(own_key, shape, cuts, least, high):
    gain, own = 1.0, jax.random.fold_in(own_key, 6)
    for axis_at, parts in cuts:
        steps = jnp.exp(jax.random.uniform(jax.random.fold_in(own, axis_at), (parts,), jnp.float32, least / len(cuts), high / len(cuts)))
        gain = gain * jnp.repeat(steps, shape[axis_at] // parts).reshape([-1 if axis == axis_at else 1 for axis in range(len(shape))])
    return gain


def scatter_about(key, dims, spread, limit, shards=(), held_as=jnp.bfloat16):
    factor_of = steps_of(key, dims, shards, -0.22, 0.18) if shards else 1.0
    result = jax.random.normal(key, dims, jnp.float32) * spread * factor_of
    return jnp.minimum(jnp.maximum(result, -limit), limit).astype(held_as)


def setup_inputs(seed: int = 0, part: int = 0) -> dict:
    key_list = jax.random.split(jax.random.key(seed), 6)
    part_keys = jax.random.split(jax.random.fold_in(key_list[5], part), 6)
    queries = scatter_about(part_keys[0], (TOKENS, HD), 1.5, 6.0, ((0, 32),))
    keys = scatter_about(part_keys[1], (TOKENS, HD), 1.5, 6.0, ((0, 32),))
    values = scatter_about(part_keys[2], (TOKENS, HD), 1.0, 6.0, ((0, 32),))
    out_weight = scatter_about(key_list[3], (HD, D), HD ** -0.5, 0.125)
    out_grad = scatter_about(part_keys[4], (TOKENS, D), 1.0, 6.0, ((0, 32),))
    return {"queries": queries, "keys": keys, "values": values, "out_weight": out_weight, "out_grad": out_grad}


def feature(x):
    return jax.nn.elu(x) + 1.0

def attend_block(query_f, key_f, value_f, state, zsum):
    block_len = query_f.shape[0]
    fq = feature(query_f.reshape(block_len, HEADS, HEAD))
    fk = feature(key_f.reshape(block_len, HEADS, HEAD))
    vv = value_f.reshape(block_len, HEADS, HEAD)
    rows = lax.broadcasted_iota(jnp.int32, (block_len, block_len), 0)
    cols = lax.broadcasted_iota(jnp.int32, (block_len, block_len), 1)
    causal = (cols <= rows).astype(jnp.float32)
    scores = jnp.einsum('thd,shd->hts', fq, fk, precision=lax.Precision.HIGHEST) * causal[None]
    numer = jnp.einsum('hts,she->the', scores, vv, precision=lax.Precision.HIGHEST)
    numer = numer + jnp.einsum('thd,hde->the', fq, state, precision=lax.Precision.HIGHEST)
    denom = lax.optimization_barrier(jnp.sum(scores, axis=2)).T + jnp.einsum('thd,hd->th', fq, zsum, precision=lax.Precision.HIGHEST)
    return (numer / denom[:, :, None]).reshape(block_len, HEADS * HEAD)

def forward(query_f, key_f, value_f):
    count = TOKENS // TOK_DEV
    qb = query_f.reshape(count, TOK_DEV, HEADS * HEAD)
    kb = key_f.reshape(count, TOK_DEV, HEADS * HEAD)
    vb = value_f.reshape(count, TOK_DEV, HEADS * HEAD)

    def step(carry, pieces):
        state, zsum = carry
        qp, kp, vp = pieces
        out = attend_block(qp, kp, vp, state, zsum)
        fk = feature(kp.reshape(TOK_DEV, HEADS, HEAD))
        vv = vp.reshape(TOK_DEV, HEADS, HEAD)
        state = state + jnp.einsum('thd,the->hde', fk, vv, precision=lax.Precision.HIGHEST)
        zsum = zsum + lax.optimization_barrier(jnp.sum(fk, axis=0))
        return ((state, zsum), out)
    init = (jnp.zeros((HEADS, HEAD, HEAD), jnp.float32), jnp.zeros((HEADS, HEAD), jnp.float32))
    _, outs = lax.scan(step, init, (qb, kb, vb))
    return outs.reshape(TOKENS, HEADS * HEAD)

def reference(queries, keys, values, out_weight, out_grad):
    query_f = queries.astype(jnp.float32)
    key_f = keys.astype(jnp.float32)
    value_f = values.astype(jnp.float32)
    attended, pullback = jax.vjp(forward, query_f, key_f, value_f)
    rounded = attended.astype(jnp.bfloat16)
    attended_grad = jnp.dot(out_grad, out_weight.T, preferred_element_type=jnp.float32)
    weight_grad = jnp.dot(rounded.T, out_grad, preferred_element_type=jnp.float32)
    query_grad, key_grad, value_grad = pullback(attended_grad)
    return (query_grad.astype(jnp.bfloat16), key_grad.astype(jnp.bfloat16), value_grad.astype(jnp.bfloat16), weight_grad)
```

```python
import functools

import jax
import jax.numpy as jnp
from jax import lax
from jax.experimental import pallas as pl
from jax.experimental.pallas import tpu as pltpu
from jax.sharding import PartitionSpec as P

HEAD = 128
MESH = pl.DeviceIdType.MESH
BF = jnp.bfloat16
F32 = jnp.float32
NN = (((1,), (0,)), ((), ()))
NT = (((1,), (1,)), ((), ()))
TN = (((0,), (0,)), ((), ()))


def split(x):
    if isinstance(x, tuple):
        return x
    if x.dtype == BF:
        return (x,)
    high = x.astype(BF)
    return (high, (x - high.astype(F32)).astype(BF))


def mm(a, b, dims):
    a, b = split(a), split(b)
    total = lax.dot_general(a[0], b[0], dims, preferred_element_type=F32)
    if len(a) > 1:
        total += lax.dot_general(a[1], b[0], dims, preferred_element_type=F32)
    if len(b) > 1:
        total += lax.dot_general(a[0], b[1], dims, preferred_element_type=F32)
    return total


def bits_of(n):
    count = n.bit_length() - 1
    assert 1 << count == n
    return count


def partner_of(me, k):
    return me + (1 - 2 * ((me // (1 << k)) % 2)) * (1 << k)


def scan_kernel(n, reverse, x_ref, e_ref, tot, recv, near, out, su, ru, sd, rd):
    me = lax.axis_index("seq")
    levels = bits_of(n)
    rows = x_ref.shape[0]
    barrier = pltpu.get_barrier_semaphore()
    for k in range(levels):
        pl.semaphore_signal(barrier, inc=1, device_id={"seq": partner_of(me, k)}, device_id_type=MESH)
    pl.semaphore_wait(barrier, levels)
    base = 0
    keeps = []
    for k in range(levels):
        half = rows >> (k + 1)
        off = rows - (rows >> k)
        bit = (me // (1 << k)) % 2
        keep = pl.multiple_of(base + bit * half, 8)
        give = pl.multiple_of(base + (1 - bit) * half, 8)
        src = x_ref if k == 0 else tot
        buf = recv.at[pl.ds(off, half)]
        copy = pltpu.make_async_remote_copy(
            src_ref=src.at[pl.ds(give, half)], dst_ref=buf, send_sem=su.at[k], recv_sem=ru.at[k],
            device_id={"seq": partner_of(me, k)}, device_id_type=MESH)
        copy.start()
        copy.wait()
        mine = src[pl.ds(keep, half), :]
        theirs = recv[pl.ds(off, half), :]
        first = jnp.where(bit == (1 if reverse else 0), mine, theirs)
        near[pl.ds(off, half), :] = first
        if k + 1 < levels:
            tot[pl.ds(keep, half), :] = mine + theirs
        keeps.append((keep, half, off, bit))
        base = keep
    e_ref[pl.ds(base, rows >> levels), :] = jnp.zeros((rows >> levels, x_ref.shape[1]), F32)
    for k in reversed(range(levels)):
        keep, half, off, bit = keeps[k]
        early = bit == (1 if reverse else 0)
        now = e_ref[pl.ds(keep, half), :]
        past = now + near[pl.ds(off, half), :]
        out[pl.ds(off, half), :] = jnp.where(early, past, now)
        copy = pltpu.make_async_remote_copy(
            src_ref=out.at[pl.ds(off, half)], dst_ref=e_ref.at[pl.ds(keep, half)],
            send_sem=sd.at[k], recv_sem=rd.at[k],
            device_id={"seq": partner_of(me, k)}, device_id_type=MESH)
        copy.start()
        e_ref[pl.ds(keep, half), :] = jnp.where(early, now, past)
        copy.wait()


def entering(x, n, reverse, collective_id):
    levels = bits_of(n)
    rows, cols = x.shape
    return pl.pallas_call(
        functools.partial(scan_kernel, n, reverse),
        out_shape=jax.ShapeDtypeStruct(x.shape, F32),
        in_specs=[pl.BlockSpec(memory_space=pltpu.VMEM)],
        out_specs=pl.BlockSpec(memory_space=pltpu.VMEM),
        scratch_shapes=[pltpu.VMEM((rows, cols), F32)] * 4 + [pltpu.SemaphoreType.DMA((levels,))] * 4,
        compiler_params=pltpu.CompilerParams(
            collective_id=collective_id, has_side_effects=True, vmem_limit_bytes=24 << 20),
        cost_estimate=pl.CostEstimate(flops=0, bytes_accessed=100_000_000, transcendentals=0),
    )(x)


def features(x):
    x = x.astype(F32)
    low = jnp.exp(jnp.minimum(x, 0.0))
    return jnp.where(x > 0, x + 1.0, low), low


def with_row(block, row, pad):
    row = jnp.where(lax.broadcasted_iota(jnp.int32, (pad - HEAD, HEAD), 0) == 0, row, 0.0)
    return jnp.concatenate([block, row], axis=0)


def sum_kernel(k_ref, v_ref, x_ref):
    fk, _ = features(k_ref[...])
    x_ref[...] = with_row(mm(v_ref[...], fk, TN), jnp.sum(fk, axis=0, keepdims=True), x_ref.shape[0])


def forward_of(q, k, v, entry):
    fq, qslope = features(q)
    fk, kslope = features(k)
    t = fq.shape[0]
    causal = lax.broadcasted_iota(jnp.int32, (t, t), 1) <= lax.broadcasted_iota(jnp.int32, (t, t), 0)
    fq_s, fk_s = split(fq), split(fk)
    scores = jnp.where(causal, mm(fq_s, fk_s, NT), 0.0)
    z = entry[HEAD:HEAD + 1, :]
    den = jnp.sum(scores, axis=1, keepdims=True) + jnp.sum(fq * z, axis=1, keepdims=True)
    scores = split(scores)
    numer = mm(scores, v, NN) + mm(fq_s, entry[:HEAD, :], NT)
    inv = 1.0 / den
    return fq, fq_s, qslope, fk_s, causal, scores, z, inv, numer * inv


def attend_kernel(q_ref, k_ref, v_ref, e_ref, da_ref, r_ref, g_ref):
    fq, fq_s, _, _, _, _, _, inv, att = forward_of(q_ref[...], k_ref[...], v_ref[...], e_ref[...])
    r_ref[...] = att.astype(BF)
    dn = da_ref[...] * inv
    dden = -jnp.sum(dn * att, axis=1, keepdims=True)
    g_ref[...] = with_row(mm(dn, fq_s, TN), jnp.sum(fq * dden, axis=0, keepdims=True), g_ref.shape[0])


def local_kernel(q_ref, k_ref, v_ref, e_ref, da_ref, dq_ref, dk_ref, dv_ref):
    v = v_ref[...]
    fq, fq_s, qslope, fk_s, causal, scores, z, inv, att = forward_of(q_ref[...], k_ref[...], v, e_ref[...])
    dn = da_ref[...] * inv
    dden = -jnp.sum(dn * att, axis=1, keepdims=True)
    dn_b = split(dn)
    dp = split(jnp.where(causal, mm(dn_b, v, NT) + dden, 0.0))
    dfq = mm(dp, fk_s, NN) + mm(dn_b, e_ref[:HEAD, :], NN) + dden * z
    dq_ref[...] = (dfq * qslope).astype(BF)
    dk_ref[...] = mm(dp, fq_s, TN)
    dv_ref[...] = mm(scores, dn_b, TN)


def finish_kernel(k_ref, v_ref, g_ref, dk_ref, dv_ref, ok_ref, ov_ref):
    fk, kslope = features(k_ref[...])
    g = split(g_ref[:HEAD, :])
    dfk = dk_ref[...] + mm(v_ref[...], g, NN) + g_ref[HEAD:HEAD + 1, :]
    ok_ref[...] = (dfk * kslope).astype(BF)
    ov_ref[...] = (dv_ref[...] + mm(fk, g, NT)).astype(BF)


def per_head(kernel, heads, tokens, pad, ins, outs, args):
    spec = {
        "t": pl.BlockSpec((tokens, HEAD), lambda h: (0, h)),
        "s": pl.BlockSpec((pad, HEAD), lambda h: (h, 0)),
    }
    shape = {"t": (tokens, heads * HEAD), "s": (heads * pad, HEAD)}
    return pl.pallas_call(
        kernel,
        grid=(heads,),
        in_specs=[spec[i] for i in ins],
        out_specs=[spec[o] for o, _ in outs],
        out_shape=[jax.ShapeDtypeStruct(shape[o], d) for o, d in outs],
        compiler_params=pltpu.CompilerParams(vmem_limit_bytes=32 << 20),
        cost_estimate=pl.CostEstimate(
            flops=heads * 8 * tokens * tokens * HEAD, bytes_accessed=8 * tokens * heads * HEAD, transcendentals=0),
    )(*args)


def body(queries, keys, values, out_weight, out_grad):
    n = lax.axis_size("seq")
    tokens, width = queries.shape
    heads = width // HEAD
    pad = HEAD + 8
    while (heads * pad) % (8 * n):
        pad += 8
    run = functools.partial(per_head, heads=heads, tokens=tokens, pad=pad)
    (part,) = run(sum_kernel, ins="tt", outs=[("s", F32)], args=(keys, values))
    entry = entering(part, n, False, 1)
    attended_grad = lax.dot_general(out_grad, out_weight, NT, preferred_element_type=F32)
    rounded, part_grad = run(
        attend_kernel, ins="tttst", outs=[("t", BF), ("s", F32)],
        args=(queries, keys, values, entry, attended_grad))
    weight_grad = lax.psum_scatter(
        lax.dot_general(rounded, out_grad, TN, preferred_element_type=F32),
        "seq", scatter_dimension=0, tiled=True)
    later = entering(part_grad, n, True, 2)
    query_grad, key_part, value_part = run(
        local_kernel, ins="tttst", outs=[("t", BF), ("t", F32), ("t", F32)],
        args=(queries, keys, values, entry, attended_grad))
    key_grad, value_grad = run(
        finish_kernel, ins="ttstt", outs=[("t", BF), ("t", BF)],
        args=(keys, values, later, key_part, value_part))
    return (query_grad, key_grad, value_grad, weight_grad)


def solution(mesh):
    rows = P(("groups", "seq"), None)
    return jax.shard_map(
        body, mesh=mesh, in_specs=(rows, rows, rows, P(), rows),
        out_specs=(rows, rows, rows, rows), check_vma=False)
```

```python
import functools

import jax
import jax.numpy as jnp
from jax import lax
from jax.experimental import pallas as pl
from jax.experimental.pallas import tpu as pltpu
from jax.sharding import PartitionSpec as P

HEAD = 128
MESH = pl.DeviceIdType.MESH
BF = jnp.bfloat16
F32 = jnp.float32
NN = (((1,), (0,)), ((), ()))
NT = (((1,), (1,)), ((), ()))
TN = (((0,), (0,)), ((), ()))


def split(x):
    if isinstance(x, tuple):
        return x
    if x.dtype == BF:
        return (x,)
    high = x.astype(BF)
    return (high, (x - high.astype(F32)).astype(BF))


def mm(a, b, dims):
    a, b = split(a), split(b)
    total = lax.dot_general(a[0], b[0], dims, preferred_element_type=F32)
    if len(a) > 1:
        total += lax.dot_general(a[1], b[0], dims, preferred_element_type=F32)
    if len(b) > 1:
        total += lax.dot_general(a[0], b[1], dims, preferred_element_type=F32)
    return total


def bits_of(n):
    count = n.bit_length() - 1
    assert 1 << count == n
    return count


def partner_of(me, k):
    return me + (1 - 2 * ((me // (1 << k)) % 2)) * (1 << k)


def sweep_up(n, reverse, x_ref, tot, recv, near, su, ru):
    me = lax.axis_index("seq")
    rows = x_ref.shape[0]
    base = 0
    keeps = []
    levels = bits_of(n)
    for k in range(levels):
        half = rows >> (k + 1)
        off = rows - (rows >> k)
        bit = (me // (1 << k)) % 2
        keep = pl.multiple_of(base + bit * half, 8)
        give = pl.multiple_of(base + (1 - bit) * half, 8)
        src = x_ref if k == 0 else tot
        copy = pltpu.make_async_remote_copy(
            src_ref=src.at[pl.ds(give, half)], dst_ref=recv.at[pl.ds(off, half)],
            send_sem=su.at[k], recv_sem=ru.at[k],
            device_id={"seq": partner_of(me, k)}, device_id_type=MESH)
        copy.start()
        copy.wait()
        mine = src[pl.ds(keep, half), :]
        theirs = recv[pl.ds(off, half), :]
        near[pl.ds(off, half), :] = jnp.where(bit == (1 if reverse else 0), mine, theirs)
        if k + 1 < levels:
            tot[pl.ds(keep, half), :] = mine + theirs
        keeps.append((keep, half, off, bit))
        base = keep
    return keeps


def sweep_down(keeps, reverse, e_ref, near, out, sd, rd):
    me = lax.axis_index("seq")
    keep, half, _, _ = keeps[-1]
    e_ref[pl.ds(keep, half), :] = jnp.zeros((half, e_ref.shape[1]), F32)
    for k in reversed(range(len(keeps))):
        keep, half, off, bit = keeps[k]
        early = bit == (1 if reverse else 0)
        now = e_ref[pl.ds(keep, half), :]
        past = now + near[pl.ds(off, half), :]
        out[pl.ds(off, half), :] = jnp.where(early, past, now)
        copy = pltpu.make_async_remote_copy(
            src_ref=out.at[pl.ds(off, half)], dst_ref=e_ref.at[pl.ds(keep, half)],
            send_sem=sd.at[k], recv_sem=rd.at[k],
            device_id={"seq": partner_of(me, k)}, device_id_type=MESH)
        copy.start()
        e_ref[pl.ds(keep, half), :] = jnp.where(early, now, past)
        copy.wait()


def greet(peers):
    barrier = pltpu.get_barrier_semaphore()
    for peer in peers:
        pl.semaphore_signal(barrier, inc=1, device_id={"seq": peer}, device_id_type=MESH)
    pl.semaphore_wait(barrier, len(peers))


def scan_kernel(n, x_ref, e_ref, tot, recv, near, out, su, ru, sd, rd):
    me = lax.axis_index("seq")
    greet([partner_of(me, k) for k in range(bits_of(n))])
    keeps = sweep_up(n, False, x_ref, tot, recv, near, su, ru)
    sweep_down(keeps, False, e_ref, near, out, sd, rd)


def scan_scratch(n, shape):
    return [pltpu.VMEM(shape, F32)] * 4 + [pltpu.SemaphoreType.DMA((bits_of(n),))] * 4


def entering(x, n):
    return pl.pallas_call(
        functools.partial(scan_kernel, n),
        out_shape=jax.ShapeDtypeStruct(x.shape, F32),
        in_specs=[pl.BlockSpec(memory_space=pltpu.VMEM)],
        out_specs=pl.BlockSpec(memory_space=pltpu.VMEM),
        scratch_shapes=scan_scratch(n, x.shape),
        compiler_params=pltpu.CompilerParams(
            collective_id=1, has_side_effects=True, vmem_limit_bytes=24 << 20),
        cost_estimate=pl.CostEstimate(flops=0, bytes_accessed=100_000_000, transcendentals=0),
    )(x)


def grads_kernel(n, plane, x_ref, r_ref, og_ref, e_ref, w_ref, tot, recv, near, out, su, ru, sd, rd,
                 og, rt, part, zr, so, sp, rp, sz, rz):
    me = lax.axis_index("seq")
    layers = n // plane
    spot, layer = me % plane, me // plane
    tokens = r_ref.shape[3]
    load = pltpu.make_async_copy(og_ref, og, so)
    load.start()
    near_peers = [layer * plane + (spot + j) % plane for j in range(1, plane)]
    far_peers = [((layer + j) % layers) * plane + spot for j in range(1, layers)]
    greet(near_peers + far_peers)
    swaps = []
    for j in range(1, plane):
        copy = pltpu.make_async_remote_copy(
            src_ref=r_ref.at[:, (spot + j) % plane], dst_ref=rt.at[j],
            send_sem=sp.at[j], recv_sem=rp.at[j],
            device_id={"seq": near_peers[j - 1]}, device_id_type=MESH)
        copy.start()
        swaps.append(copy)
    keeps = sweep_up(n, True, x_ref, tot, recv, near, su, ru)
    rt[0] = r_ref[:, spot]
    load.wait()
    for copy in swaps:
        copy.wait()
    step = 512

    def columns(c, carry):
        cols = pl.ds(pl.multiple_of(c * step, step), step)
        acc = None
        for j in range(plane):
            rows = pl.ds(pl.multiple_of(((spot - j + plane) % plane) * tokens, tokens), tokens)
            left = rt[j].reshape(layers * rt.shape[2], tokens).astype(BF)
            term = lax.dot_general(left, og[rows, cols].astype(BF), NN, preferred_element_type=F32)
            acc = term if acc is None else acc + term
        part[:, :, cols] = acc.reshape(layers, rt.shape[2], step)
        return carry

    lax.fori_loop(0, og.shape[1] // step, columns, 0)
    sums = []
    for j in range(1, layers):
        copy = pltpu.make_async_remote_copy(
            src_ref=part.at[(layer + j) % layers], dst_ref=zr.at[j],
            send_sem=sz.at[j], recv_sem=rz.at[j],
            device_id={"seq": far_peers[j - 1]}, device_id_type=MESH)
        copy.start()
        sums.append(copy)
    sweep_down(keeps, True, e_ref, near, out, sd, rd)
    for copy in sums:
        copy.wait()
    total = part[layer]
    for j in range(1, layers):
        total = total + zr[j]
    w_ref[...] = total


def gradients(x, turned, og, n, plane):
    layers = n // plane
    rows, tokens = turned.shape
    width = og.shape[1]
    mine = rows // n
    vm = pl.BlockSpec(memory_space=pltpu.VMEM)
    dma = pltpu.SemaphoreType.DMA
    return pl.pallas_call(
        functools.partial(grads_kernel, n, plane),
        out_shape=[jax.ShapeDtypeStruct(x.shape, F32), jax.ShapeDtypeStruct((mine, width), F32)],
        in_specs=[vm, vm, pl.BlockSpec(memory_space=pl.ANY)],
        out_specs=[vm, vm],
        scratch_shapes=scan_scratch(n, x.shape) + [
            pltpu.VMEM(og.shape, F32), pltpu.VMEM((plane, layers, mine, tokens), F32),
            pltpu.VMEM((layers, mine, width), F32), pltpu.VMEM((layers, mine, width), F32),
            dma, dma((plane,)), dma((plane,)), dma((layers,)), dma((layers,))],
        compiler_params=pltpu.CompilerParams(
            collective_id=2, has_side_effects=True, vmem_limit_bytes=48 << 20),
        cost_estimate=pl.CostEstimate(flops=0, bytes_accessed=200_000_000, transcendentals=0),
    )(x, turned.reshape(layers, plane, mine, tokens), og)


def features(x):
    x = x.astype(F32)
    low = jnp.exp(jnp.minimum(x, 0.0))
    return jnp.where(x > 0, x + 1.0, low), low


def with_row(block, row, pad):
    row = jnp.where(lax.broadcasted_iota(jnp.int32, (pad - HEAD, HEAD), 0) == 0, row, 0.0)
    return jnp.concatenate([block, row], axis=0)


def sum_kernel(k_ref, v_ref, x_ref):
    fk, _ = features(k_ref[...])
    x_ref[...] = with_row(mm(v_ref[...], fk, TN), jnp.sum(fk, axis=0, keepdims=True), x_ref.shape[0])


def forward_of(q, k, v, entry):
    fq, qslope = features(q)
    fk, kslope = features(k)
    t = fq.shape[0]
    causal = lax.broadcasted_iota(jnp.int32, (t, t), 1) <= lax.broadcasted_iota(jnp.int32, (t, t), 0)
    fq_s, fk_s = split(fq), split(fk)
    scores = jnp.where(causal, mm(fq_s, fk_s, NT), 0.0)
    z = entry[HEAD:HEAD + 1, :]
    den = jnp.sum(scores, axis=1, keepdims=True) + jnp.sum(fq * z, axis=1, keepdims=True)
    scores = split(scores)
    numer = mm(scores, v, NN) + mm(fq_s, entry[:HEAD, :], NT)
    inv = 1.0 / den
    return fq, fq_s, qslope, fk_s, causal, scores, z, inv, numer * inv


def attend_kernel(q_ref, k_ref, v_ref, e_ref, da_ref, r_ref, g_ref):
    fq, fq_s, _, _, _, _, _, inv, att = forward_of(q_ref[...], k_ref[...], v_ref[...], e_ref[...])
    r_ref[...] = att.T
    dn = da_ref[...] * inv
    dden = -jnp.sum(dn * att, axis=1, keepdims=True)
    g_ref[...] = with_row(mm(dn, fq_s, TN), jnp.sum(fq * dden, axis=0, keepdims=True), g_ref.shape[0])


def local_kernel(q_ref, k_ref, v_ref, e_ref, da_ref, dq_ref, dk_ref, dv_ref):
    v = v_ref[...]
    fq, fq_s, qslope, fk_s, causal, scores, z, inv, att = forward_of(q_ref[...], k_ref[...], v, e_ref[...])
    dn = da_ref[...] * inv
    dden = -jnp.sum(dn * att, axis=1, keepdims=True)
    dn_b = split(dn)
    dp = split(jnp.where(causal, mm(dn_b, v, NT) + dden, 0.0))
    dfq = mm(dp, fk_s, NN) + mm(dn_b, e_ref[:HEAD, :], NN) + dden * z
    dq_ref[...] = (dfq * qslope).astype(BF)
    dk_ref[...] = mm(dp, fq_s, TN)
    dv_ref[...] = mm(scores, dn_b, TN)


def finish_kernel(k_ref, v_ref, g_ref, dk_ref, dv_ref, ok_ref, ov_ref):
    fk, kslope = features(k_ref[...])
    g = split(g_ref[:HEAD, :])
    dfk = dk_ref[...] + mm(v_ref[...], g, NN) + g_ref[HEAD:HEAD + 1, :]
    ok_ref[...] = (dfk * kslope).astype(BF)
    ov_ref[...] = (dv_ref[...] + mm(fk, g, NT)).astype(BF)


def per_head(kernel, heads, tokens, pad, ins, outs, args):
    spec = {
        "t": pl.BlockSpec((tokens, HEAD), lambda h: (0, h)),
        "s": pl.BlockSpec((pad, HEAD), lambda h: (h, 0)),
        "r": pl.BlockSpec((HEAD, tokens), lambda h: (h, 0)),
    }
    shape = {"t": (tokens, heads * HEAD), "s": (heads * pad, HEAD), "r": (heads * HEAD, tokens)}
    return pl.pallas_call(
        kernel,
        grid=(heads,),
        in_specs=[spec[i] for i in ins],
        out_specs=[spec[o] for o, _ in outs],
        out_shape=[jax.ShapeDtypeStruct(shape[o], d) for o, d in outs],
        compiler_params=pltpu.CompilerParams(vmem_limit_bytes=32 << 20),
        cost_estimate=pl.CostEstimate(
            flops=heads * 8 * tokens * tokens * HEAD, bytes_accessed=8 * tokens * heads * HEAD, transcendentals=0),
    )(*args)


def body(queries, keys, values, out_weight, out_grad):
    n = lax.axis_size("seq")
    tokens, width = queries.shape
    heads = width // HEAD
    pad = HEAD + 8
    while (heads * pad) % (8 * n):
        pad += 8
    run = functools.partial(per_head, heads=heads, tokens=tokens, pad=pad)
    plane = min(8, n)
    blocks = [list(range(at, at + plane)) for at in range(0, n, plane)]
    gathered = lax.all_gather(out_grad.astype(F32), "seq", axis_index_groups=blocks, tiled=True)
    (part,) = run(sum_kernel, ins="tt", outs=[("s", F32)], args=(keys, values))
    entry = entering(part, n)
    attended_grad = lax.dot_general(out_grad, out_weight, NT, preferred_element_type=F32)
    turned, part_grad = run(
        attend_kernel, ins="tttst", outs=[("r", F32), ("s", F32)],
        args=(queries, keys, values, entry, attended_grad))
    query_grad, key_part, value_part = run(
        local_kernel, ins="tttst", outs=[("t", BF), ("t", F32), ("t", F32)],
        args=(queries, keys, values, entry, attended_grad))
    later, weight_grad = gradients(part_grad, turned, gathered, n, plane)
    key_grad, value_grad = run(
        finish_kernel, ins="ttstt", outs=[("t", BF), ("t", BF)],
        args=(keys, values, later, key_part, value_part))
    return (query_grad, key_grad, value_grad, weight_grad)


def solution(mesh):
    rows = P(("groups", "seq"), None)
    return jax.shard_map(
        body, mesh=mesh, in_specs=(rows, rows, rows, P(), rows),
        out_specs=(rows, rows, rows, rows), check_vma=False)
```

```python
import functools

import jax
import jax.numpy as jnp
from jax import lax
from jax.experimental import pallas as pl
from jax.experimental.pallas import tpu as pltpu
from jax.sharding import PartitionSpec as P

HEAD = 128
MESH = pl.DeviceIdType.MESH
BF = jnp.bfloat16
F32 = jnp.float32
NN = (((1,), (0,)), ((), ()))
NT = (((1,), (1,)), ((), ()))
TN = (((0,), (0,)), ((), ()))


def split(x):
    if isinstance(x, tuple):
        return x
    if x.dtype == BF:
        return (x,)
    high = x.astype(BF)
    return (high, (x - high.astype(F32)).astype(BF))


def mm(a, b, dims):
    a, b = split(a), split(b)
    total = lax.dot_general(a[0], b[0], dims, preferred_element_type=F32)
    if len(a) > 1:
        total += lax.dot_general(a[1], b[0], dims, preferred_element_type=F32)
    if len(b) > 1:
        total += lax.dot_general(a[0], b[1], dims, preferred_element_type=F32)
    return total


def bits_of(n):
    count = n.bit_length() - 1
    assert 1 << count == n
    return count


def partner_of(me, k):
    return me + (1 - 2 * ((me // (1 << k)) % 2)) * (1 << k)


def sweep_up(n, reverse, x_ref, tot, recv, near, su, ru):
    me = lax.axis_index("seq")
    rows = x_ref.shape[0]
    base = 0
    keeps = []
    levels = bits_of(n)
    for k in range(levels):
        half = rows >> (k + 1)
        off = rows - (rows >> k)
        bit = (me // (1 << k)) % 2
        keep = pl.multiple_of(base + bit * half, 8)
        give = pl.multiple_of(base + (1 - bit) * half, 8)
        src = x_ref if k == 0 else tot
        copy = pltpu.make_async_remote_copy(
            src_ref=src.at[pl.ds(give, half)], dst_ref=recv.at[pl.ds(off, half)],
            send_sem=su.at[k], recv_sem=ru.at[k],
            device_id={"seq": partner_of(me, k)}, device_id_type=MESH)
        copy.start()
        copy.wait()
        mine = src[pl.ds(keep, half), :]
        theirs = recv[pl.ds(off, half), :]
        near[pl.ds(off, half), :] = jnp.where(bit == (1 if reverse else 0), mine, theirs)
        if k + 1 < levels:
            tot[pl.ds(keep, half), :] = mine + theirs
        keeps.append((keep, half, off, bit))
        base = keep
    return keeps


def sweep_down(keeps, bits, reverse, e_ref, near, out, sd, rd):
    me = lax.axis_index("seq")
    if len(keeps) - 1 in bits:
        keep, half, _, _ = keeps[-1]
        e_ref[pl.ds(keep, half), :] = jnp.zeros((half, e_ref.shape[1]), F32)
    for k in reversed(bits):
        keep, half, off, bit = keeps[k]
        early = bit == (1 if reverse else 0)
        now = e_ref[pl.ds(keep, half), :]
        past = now + near[pl.ds(off, half), :]
        out[pl.ds(off, half), :] = jnp.where(early, past, now)
        copy = pltpu.make_async_remote_copy(
            src_ref=out.at[pl.ds(off, half)], dst_ref=e_ref.at[pl.ds(keep, half)],
            send_sem=sd.at[k], recv_sem=rd.at[k],
            device_id={"seq": partner_of(me, k)}, device_id_type=MESH)
        copy.start()
        e_ref[pl.ds(keep, half), :] = jnp.where(early, now, past)
        copy.wait()


def greet(peers):
    barrier = pltpu.get_barrier_semaphore()
    for peer in peers:
        pl.semaphore_signal(barrier, inc=1, device_id={"seq": peer}, device_id_type=MESH)
    pl.semaphore_wait(barrier, len(peers))


def scan_kernel(n, x_ref, e_ref, tot, recv, near, out, su, ru, sd, rd):
    me = lax.axis_index("seq")
    greet([partner_of(me, k) for k in range(bits_of(n))])
    keeps = sweep_up(n, False, x_ref, tot, recv, near, su, ru)
    sweep_down(keeps, range(len(keeps)), False, e_ref, near, out, sd, rd)


def scan_scratch(n, shape):
    return [pltpu.VMEM(shape, F32)] * 4 + [pltpu.SemaphoreType.DMA((bits_of(n),))] * 4


def entering(x, n):
    return pl.pallas_call(
        functools.partial(scan_kernel, n),
        out_shape=jax.ShapeDtypeStruct(x.shape, F32),
        in_specs=[pl.BlockSpec(memory_space=pltpu.VMEM)],
        out_specs=pl.BlockSpec(memory_space=pltpu.VMEM),
        scratch_shapes=scan_scratch(n, x.shape),
        compiler_params=pltpu.CompilerParams(
            collective_id=1, has_side_effects=True, vmem_limit_bytes=24 << 20),
        cost_estimate=pl.CostEstimate(flops=0, bytes_accessed=100_000_000, transcendentals=0),
    )(x)


def grads_kernel(n, plane, x_ref, r_ref, og_ref, q_ref, k_ref, v_ref, en_ref, da_ref,
                 dq_ref, dk_ref, dv_ref, w_ref, tot, recv, near, out, su, ru, sd, rd,
                 e_ref, og, rt, part, zr, so, sp, rp, sz, rz):
    me = lax.axis_index("seq")
    layers = n // plane
    spot, layer = me % plane, me // plane
    tokens = r_ref.shape[3]
    load = pltpu.make_async_copy(og_ref, og, so)
    load.start()
    near_peers = [layer * plane + (spot + j) % plane for j in range(1, plane)]
    far_peers = [((layer + j) % layers) * plane + spot for j in range(1, layers)]
    greet(near_peers + far_peers)
    swaps = []
    for j in range(1, plane):
        copy = pltpu.make_async_remote_copy(
            src_ref=r_ref.at[:, (spot + j) % plane], dst_ref=rt.at[j],
            send_sem=sp.at[j], recv_sem=rp.at[j],
            device_id={"seq": near_peers[j - 1]}, device_id_type=MESH)
        copy.start()
        swaps.append(copy)
    keeps = sweep_up(n, True, x_ref, tot, recv, near, su, ru)
    rt[0] = r_ref[:, spot]
    load.wait()
    for copy in swaps:
        copy.wait()
    step = 512

    def columns(c, carry):
        cols = pl.ds(pl.multiple_of(c * step, step), step)
        acc = None
        for j in range(plane):
            rows = pl.ds(pl.multiple_of(((spot - j + plane) % plane) * tokens, tokens), tokens)
            left = rt[j].reshape(layers * rt.shape[2], tokens).astype(BF)
            term = lax.dot_general(left, og[rows, cols].astype(BF), NN, preferred_element_type=F32)
            acc = term if acc is None else acc + term
        part[:, :, cols] = acc.reshape(layers, rt.shape[2], step)
        return carry

    lax.fori_loop(0, og.shape[1] // step, columns, 0)
    low = bits_of(plane)
    sweep_down(keeps, range(low, len(keeps)), True, e_ref, near, out, sd, rd)
    sums = []
    for j in range(1, layers):
        copy = pltpu.make_async_remote_copy(
            src_ref=part.at[(layer + j) % layers], dst_ref=zr.at[j],
            send_sem=sz.at[j], recv_sem=rz.at[j],
            device_id={"seq": far_peers[j - 1]}, device_id_type=MESH)
        copy.start()
        sums.append(copy)
    sweep_down(keeps, range(low), True, e_ref, near, out, sd, rd)
    heads = q_ref.shape[1] // HEAD
    pad = x_ref.shape[0] // heads

    def head(h, carry):
        cols = pl.ds(pl.multiple_of(h * HEAD, HEAD), HEAD)
        block = pl.ds(pl.multiple_of(h * pad, 8), pad)
        dq_ref[:, cols], dk_ref[:, cols], dv_ref[:, cols] = gradients_of(
            q_ref[:, cols], k_ref[:, cols], v_ref[:, cols], en_ref[block, :], da_ref[:, cols], e_ref[block, :])
        return carry

    lax.fori_loop(0, heads, head, 0)
    for copy in sums:
        copy.wait()
    total = part[layer]
    for j in range(1, layers):
        total = total + zr[j]
    w_ref[...] = total


def gradients(x, turned, og, queries, keys, values, entry, attended_grad, n, plane):
    layers = n // plane
    rows, tokens = turned.shape
    width = og.shape[1]
    mine = rows // n
    vm = pl.BlockSpec(memory_space=pltpu.VMEM)
    dma = pltpu.SemaphoreType.DMA
    return pl.pallas_call(
        functools.partial(grads_kernel, n, plane),
        out_shape=[jax.ShapeDtypeStruct(queries.shape, BF)] * 3 + [jax.ShapeDtypeStruct((mine, width), F32)],
        in_specs=[vm, vm, pl.BlockSpec(memory_space=pl.ANY)] + [vm] * 5,
        out_specs=[vm] * 4,
        scratch_shapes=scan_scratch(n, x.shape) + [
            pltpu.VMEM(x.shape, F32),
            pltpu.VMEM(og.shape, F32), pltpu.VMEM((plane, layers, mine, tokens), F32),
            pltpu.VMEM((layers, mine, width), F32), pltpu.VMEM((layers, mine, width), F32),
            dma, dma((plane,)), dma((plane,)), dma((layers,)), dma((layers,))],
        compiler_params=pltpu.CompilerParams(
            collective_id=2, has_side_effects=True, vmem_limit_bytes=48 << 20),
        cost_estimate=pl.CostEstimate(flops=0, bytes_accessed=200_000_000, transcendentals=0),
    )(x, turned.reshape(layers, plane, mine, tokens), og, queries, keys, values, entry, attended_grad)


def features(x):
    x = x.astype(F32)
    low = jnp.exp(jnp.minimum(x, 0.0))
    return jnp.where(x > 0, x + 1.0, low), low


def with_row(block, row, pad):
    row = jnp.where(lax.broadcasted_iota(jnp.int32, (pad - HEAD, HEAD), 0) == 0, row, 0.0)
    return jnp.concatenate([block, row], axis=0)


def sum_kernel(k_ref, v_ref, x_ref):
    fk, _ = features(k_ref[...])
    x_ref[...] = with_row(mm(v_ref[...], fk, TN), jnp.sum(fk, axis=0, keepdims=True), x_ref.shape[0])


def forward_of(q, k, v, entry):
    fq, qslope = features(q)
    fk, kslope = features(k)
    t = fq.shape[0]
    causal = lax.broadcasted_iota(jnp.int32, (t, t), 1) <= lax.broadcasted_iota(jnp.int32, (t, t), 0)
    fq_s, fk_s = split(fq), split(fk)
    scores = jnp.where(causal, mm(fq_s, fk_s, NT), 0.0)
    z = entry[HEAD:HEAD + 1, :]
    den = jnp.sum(scores, axis=1, keepdims=True) + jnp.sum(fq * z, axis=1, keepdims=True)
    scores = split(scores)
    numer = mm(scores, v, NN) + mm(fq_s, entry[:HEAD, :], NT)
    inv = 1.0 / den
    return fq, fq_s, qslope, fk_s, causal, scores, z, inv, numer * inv


def attend_kernel(q_ref, k_ref, v_ref, e_ref, da_ref, r_ref, g_ref):
    fq, fq_s, _, _, _, _, _, inv, att = forward_of(q_ref[...], k_ref[...], v_ref[...], e_ref[...])
    r_ref[...] = att.T
    dn = da_ref[...] * inv
    dden = -jnp.sum(dn * att, axis=1, keepdims=True)
    g_ref[...] = with_row(mm(dn, fq_s, TN), jnp.sum(fq * dden, axis=0, keepdims=True), g_ref.shape[0])


def gradients_of(q, k, v, entry, da, later):
    fq, fq_s, qslope, fk_s, causal, scores, z, inv, att = forward_of(q, k, v, entry)
    kslope = jnp.where(k.astype(F32) > 0, 1.0, jnp.exp(jnp.minimum(k.astype(F32), 0.0)))
    dn = da * inv
    dden = -jnp.sum(dn * att, axis=1, keepdims=True)
    dn_s = split(dn)
    dp = split(jnp.where(causal, mm(dn_s, v, NT) + dden, 0.0))
    g = split(later[:HEAD, :])
    dfq = mm(dp, fk_s, NN) + mm(dn_s, entry[:HEAD, :], NN) + dden * z
    dfk = mm(dp, fq_s, TN) + mm(v, g, NN) + later[HEAD:HEAD + 1, :]
    dv = mm(scores, dn_s, TN) + mm(fk_s, g, NT)
    return (dfq * qslope).astype(BF), (dfk * kslope).astype(BF), dv.astype(BF)


def per_head(kernel, heads, tokens, pad, ins, outs, args):
    spec = {
        "t": pl.BlockSpec((tokens, HEAD), lambda h: (0, h)),
        "s": pl.BlockSpec((pad, HEAD), lambda h: (h, 0)),
        "r": pl.BlockSpec((HEAD, tokens), lambda h: (h, 0)),
    }
    shape = {"t": (tokens, heads * HEAD), "s": (heads * pad, HEAD), "r": (heads * HEAD, tokens)}
    return pl.pallas_call(
        kernel,
        grid=(heads,),
        in_specs=[spec[i] for i in ins],
        out_specs=[spec[o] for o, _ in outs],
        out_shape=[jax.ShapeDtypeStruct(shape[o], d) for o, d in outs],
        compiler_params=pltpu.CompilerParams(vmem_limit_bytes=32 << 20),
        cost_estimate=pl.CostEstimate(
            flops=heads * 8 * tokens * tokens * HEAD, bytes_accessed=8 * tokens * heads * HEAD, transcendentals=0),
    )(*args)


def body(queries, keys, values, out_weight, out_grad):
    n = lax.axis_size("seq")
    tokens, width = queries.shape
    heads = width // HEAD
    pad = HEAD + 8
    while (heads * pad) % (8 * n):
        pad += 8
    run = functools.partial(per_head, heads=heads, tokens=tokens, pad=pad)
    plane = min(8, n)
    blocks = [list(range(at, at + plane)) for at in range(0, n, plane)]
    gathered = lax.all_gather(out_grad.astype(F32), "seq", axis_index_groups=blocks, tiled=True)
    (part,) = run(sum_kernel, ins="tt", outs=[("s", F32)], args=(keys, values))
    entry = entering(part, n)
    attended_grad = lax.dot_general(out_grad, out_weight, NT, preferred_element_type=F32)
    turned, part_grad = run(
        attend_kernel, ins="tttst", outs=[("r", F32), ("s", F32)],
        args=(queries, keys, values, entry, attended_grad))
    query_grad, key_grad, value_grad, weight_grad = gradients(
        part_grad, turned, gathered, queries, keys, values, entry, attended_grad, n, plane)
    return (query_grad, key_grad, value_grad, weight_grad)


def solution(mesh):
    rows = P(("groups", "seq"), None)
    return jax.shard_map(
        body, mesh=mesh, in_specs=(rows, rows, rows, P(), rows),
        out_specs=(rows, rows, rows, rows), check_vma=False)
```

```python
import functools

import jax
import jax.numpy as jnp
from jax import lax
from jax.experimental import pallas as pl
from jax.experimental.pallas import tpu as pltpu
from jax.sharding import PartitionSpec as P

HEAD = 128
MESH = pl.DeviceIdType.MESH
BF = jnp.bfloat16
F32 = jnp.float32
NN = (((1,), (0,)), ((), ()))
NT = (((1,), (1,)), ((), ()))
TN = (((0,), (0,)), ((), ()))


def split(x):
    if isinstance(x, tuple):
        return x
    if x.dtype == BF:
        return (x,)
    high = x.astype(BF)
    return (high, (x - high.astype(F32)).astype(BF))


def mm(a, b, dims):
    a, b = split(a), split(b)
    total = lax.dot_general(a[0], b[0], dims, preferred_element_type=F32)
    if len(a) > 1:
        total += lax.dot_general(a[1], b[0], dims, preferred_element_type=F32)
    if len(b) > 1:
        total += lax.dot_general(a[0], b[1], dims, preferred_element_type=F32)
    return total


def bits_of(n):
    count = n.bit_length() - 1
    assert 1 << count == n
    return count


def partner_of(me, k):
    return me + (1 - 2 * ((me // (1 << k)) % 2)) * (1 << k)


def sweep_up(n, reverse, x_ref, tot, recv, near, su, ru, work):
    me = lax.axis_index("seq")
    rows = x_ref.shape[0]
    base = 0
    levels = bits_of(n)
    for k in range(levels):
        half = rows >> (k + 1)
        off = rows - (rows >> k)
        bit = (me // (1 << k)) % 2
        keep = pl.multiple_of(base + bit * half, 8)
        give = pl.multiple_of(base + (1 - bit) * half, 8)
        src = x_ref if k == 0 else tot
        copy = pltpu.make_async_remote_copy(
            src_ref=src.at[pl.ds(give, half)], dst_ref=recv.at[pl.ds(off, half)],
            send_sem=su.at[k], recv_sem=ru.at[k],
            device_id={"seq": partner_of(me, k)}, device_id_type=MESH)
        copy.start()
        work()
        copy.wait()
        mine = src[pl.ds(keep, half), :]
        theirs = recv[pl.ds(off, half), :]
        near[pl.ds(off, half), :] = jnp.where(bit == (1 if reverse else 0), mine, theirs)
        if k + 1 < levels:
            tot[pl.ds(keep, half), :] = mine + theirs
        base = keep


def keeps_of(n, rows):
    me = lax.axis_index("seq")
    base, keeps = 0, []
    for k in range(bits_of(n)):
        half = rows >> (k + 1)
        bit = (me // (1 << k)) % 2
        base = pl.multiple_of(base + bit * half, 8)
        keeps.append((base, half, rows - (rows >> k), bit))
    return keeps


def sweep_down(keeps, bits, reverse, e_ref, near, out, sd, rd, work):
    me = lax.axis_index("seq")
    if len(keeps) - 1 in bits:
        keep, half, _, _ = keeps[-1]
        e_ref[pl.ds(keep, half), :] = jnp.zeros((half, e_ref.shape[1]), F32)
    for k in reversed(bits):
        keep, half, off, bit = keeps[k]
        early = bit == (1 if reverse else 0)
        now = e_ref[pl.ds(keep, half), :]
        past = now + near[pl.ds(off, half), :]
        out[pl.ds(off, half), :] = jnp.where(early, past, now)
        copy = pltpu.make_async_remote_copy(
            src_ref=out.at[pl.ds(off, half)], dst_ref=e_ref.at[pl.ds(keep, half)],
            send_sem=sd.at[k], recv_sem=rd.at[k],
            device_id={"seq": partner_of(me, k)}, device_id_type=MESH)
        copy.start()
        e_ref[pl.ds(keep, half), :] = jnp.where(early, now, past)
        work()
        copy.wait()


def greet(peers):
    barrier = pltpu.get_barrier_semaphore()
    for peer in peers:
        pl.semaphore_signal(barrier, inc=1, device_id={"seq": peer}, device_id_type=MESH)
    pl.semaphore_wait(barrier, len(peers))


def shares(heads, parts, one):
    left = iter(range(parts))

    def work():
        i = next(left)
        lax.fori_loop(heads * i // parts, heads * (i + 1) // parts, one, 0)

    return work


def scan_kernel(n, x_ref, og_ref, w_ref, e_ref, da_ref, tot, recv, near, out, su, ru, sd, rd):
    levels = bits_of(n)
    me = lax.axis_index("seq")

    def head(h, carry):
        at = pl.ds(pl.multiple_of(h * HEAD, HEAD), HEAD)
        da_ref[:, at] = lax.dot_general(og_ref[...], w_ref[at, :], NT, preferred_element_type=F32)
        return carry

    work = shares(w_ref.shape[0] // HEAD, 2 * levels, head)
    greet([partner_of(me, k) for k in range(levels)])
    sweep_up(n, False, x_ref, tot, recv, near, su, ru, work)
    sweep_down(keeps_of(n, x_ref.shape[0]), range(levels), False, e_ref, near, out, sd, rd, work)


def scan_scratch(n, shape):
    return [pltpu.VMEM(shape, F32)] * 4 + [pltpu.SemaphoreType.DMA((bits_of(n),))] * 4


VM = pl.BlockSpec(memory_space=pltpu.VMEM)
DMA = pltpu.SemaphoreType.DMA


def remote_call(kernel, collective_id, outs, ins, scratch, limit, args):
    return pl.pallas_call(
        kernel, out_shape=outs, in_specs=ins, out_specs=[VM] * len(outs), scratch_shapes=scratch,
        compiler_params=pltpu.CompilerParams(
            collective_id=collective_id, has_side_effects=True, vmem_limit_bytes=limit << 20),
        cost_estimate=pl.CostEstimate(flops=0, bytes_accessed=100_000_000, transcendentals=0),
    )(*args)


def swap_kernel(n, plane, x_ref, r_ref, q_ref, k_ref, v_ref, en_ref, da_ref,
                rt_ref, near, e_part, dq_ref, dk_ref, dv_ref, tot, recv, out, su, ru, sd, rd, e_ref, sp, rp):
    me = lax.axis_index("seq")
    layers = n // plane
    levels, low = bits_of(n), bits_of(plane)
    spot, layer = me % plane, me // plane
    near_peers = [layer * plane + (spot + j) % plane for j in range(1, plane)]
    far_peers = [partner_of(me, k) for k in range(low, levels)]
    greet(near_peers + far_peers)
    swaps = []
    for j in range(1, plane):
        copy = pltpu.make_async_remote_copy(
            src_ref=r_ref.at[:, (spot + j) % plane], dst_ref=rt_ref.at[j],
            send_sem=sp.at[j], recv_sem=rp.at[j],
            device_id={"seq": near_peers[j - 1]}, device_id_type=MESH)
        copy.start()
        swaps.append(copy)
    heads = q_ref.shape[1] // HEAD
    pad = x_ref.shape[0] // heads

    def head(h, carry):
        cols = pl.ds(pl.multiple_of(h * HEAD, HEAD), HEAD)
        block = pl.ds(pl.multiple_of(h * pad, 8), pad)
        dq_ref[:, cols], dk_ref[:, cols], dv_ref[:, cols] = local_of(
            q_ref[:, cols], k_ref[:, cols], v_ref[:, cols], en_ref[block, :], da_ref[:, cols])
        return carry

    work = shares(heads, 2 * levels - low, head)
    sweep_up(n, True, x_ref, tot, recv, near, su, ru, work)
    keeps = keeps_of(n, x_ref.shape[0])
    sweep_down(keeps, range(low, levels), True, e_ref, near, out, sd, rd, work)
    e_part[...] = e_ref[pl.ds(keeps[low - 1][0], e_part.shape[0]), :]
    rt_ref[0] = r_ref[:, spot]
    for copy in swaps:
        copy.wait()


def sum_out_kernel(n, plane, rt, og_ref, near, e_part, k_ref, v_ref, dkl_ref, dvl_ref,
                   dk_ref, dv_ref, w_ref, out, sd, rd, e_ref, og, part, zr, so, sz, rz):
    me = lax.axis_index("seq")
    layers = n // plane
    low = bits_of(plane)
    spot, layer = me % plane, me // plane
    tokens = rt.shape[3]
    tiles = so.shape[0]
    step = og.shape[1] // tiles
    loads = []
    for c in range(tiles):
        at = pl.ds(c * step, step)
        load = pltpu.make_async_copy(og_ref.at[:, at], og.at[:, at], so.at[c])
        load.start()
        loads.append(load)
    keeps = keeps_of(n, near.shape[0])
    e_ref[pl.ds(keeps[low - 1][0], e_part.shape[0]), :] = e_part[...]
    far_peers = [((layer + j) % layers) * plane + spot for j in range(1, layers)]
    greet(far_peers + [partner_of(me, k) for k in range(low)])
    sums = []
    for c in range(tiles):
        cols = pl.ds(c * step, step)
        loads[c].wait()
        acc = None
        for j in range(plane):
            rows = pl.ds(pl.multiple_of(((spot - j + plane) % plane) * tokens, tokens), tokens)
            left = rt[j].reshape(layers * rt.shape[2], tokens).astype(BF)
            term = lax.dot_general(left, og[rows, cols].astype(BF), NN, preferred_element_type=F32)
            acc = term if acc is None else acc + term
        part[:, :, cols] = acc.reshape(layers, rt.shape[2], step)
        for j in range(1, layers):
            copy = pltpu.make_async_remote_copy(
                src_ref=part.at[(layer + j) % layers, :, cols], dst_ref=zr.at[j, :, cols],
                send_sem=sz.at[c, j], recv_sem=rz.at[c, j],
                device_id={"seq": far_peers[j - 1]}, device_id_type=MESH)
            copy.start()
            sums.append(copy)
    sweep_down(keeps, range(low), True, e_ref, near, out, sd, rd, lambda: None)
    heads = k_ref.shape[1] // HEAD
    pad = near.shape[0] // heads

    def head(h, carry):
        cols = pl.ds(pl.multiple_of(h * HEAD, HEAD), HEAD)
        block = pl.ds(pl.multiple_of(h * pad, 8), pad)
        later = e_ref[block, :]
        fk, kslope = features(k_ref[:, cols])
        g = split(later[:HEAD, :])
        dfk = dkl_ref[:, cols] + mm(v_ref[:, cols], g, NN) + later[HEAD:HEAD + 1, :]
        dk_ref[:, cols] = (dfk * kslope).astype(BF)
        dv_ref[:, cols] = (dvl_ref[:, cols] + mm(fk, g, NT)).astype(BF)
        return carry

    lax.fori_loop(0, heads, head, 0)
    for copy in sums:
        copy.wait()
    total = part[layer]
    for j in range(1, layers):
        total = total + zr[j]
    w_ref[...] = total


def features(x):
    x = x.astype(F32)
    low = jnp.exp(jnp.minimum(x, 0.0))
    return jnp.where(x > 0, x + 1.0, low), low


def with_row(block, row, pad):
    row = jnp.where(lax.broadcasted_iota(jnp.int32, (pad - HEAD, HEAD), 0) == 0, row, 0.0)
    return jnp.concatenate([block, row], axis=0)


def sum_kernel(k_ref, v_ref, x_ref):
    fk, _ = features(k_ref[...])
    x_ref[...] = with_row(mm(v_ref[...], fk, TN), jnp.sum(fk, axis=0, keepdims=True), x_ref.shape[0])


def forward_of(q, k, v, entry):
    fq, qslope = features(q)
    fk, kslope = features(k)
    t = fq.shape[0]
    causal = lax.broadcasted_iota(jnp.int32, (t, t), 1) <= lax.broadcasted_iota(jnp.int32, (t, t), 0)
    fq_s, fk_s = split(fq), split(fk)
    scores = jnp.where(causal, mm(fq_s, fk_s, NT), 0.0)
    z = entry[HEAD:HEAD + 1, :]
    den = jnp.sum(scores, axis=1, keepdims=True) + jnp.sum(fq * z, axis=1, keepdims=True)
    scores = split(scores)
    numer = mm(scores, v, NN) + mm(fq_s, entry[:HEAD, :], NT)
    inv = 1.0 / den
    return fq, fq_s, qslope, fk_s, causal, scores, z, inv, numer * inv


def attend_kernel(q_ref, k_ref, v_ref, e_ref, da_ref, r_ref, g_ref):
    fq, fq_s, _, _, _, _, _, inv, att = forward_of(q_ref[...], k_ref[...], v_ref[...], e_ref[...])
    r_ref[...] = att.T
    dn = da_ref[...] * inv
    dden = -jnp.sum(dn * att, axis=1, keepdims=True)
    g_ref[...] = with_row(mm(dn, fq_s, TN), jnp.sum(fq * dden, axis=0, keepdims=True), g_ref.shape[0])


def local_of(q, k, v, entry, da):
    fq, fq_s, qslope, fk_s, causal, scores, z, inv, att = forward_of(q, k, v, entry)
    dn = da * inv
    dden = -jnp.sum(dn * att, axis=1, keepdims=True)
    dn_s = split(dn)
    dp = split(jnp.where(causal, mm(dn_s, v, NT) + dden, 0.0))
    dfq = mm(dp, fk_s, NN) + mm(dn_s, entry[:HEAD, :], NN) + dden * z
    return (dfq * qslope).astype(BF), mm(dp, fq_s, TN), mm(scores, dn_s, TN)


def per_head(kernel, heads, tokens, pad, ins, outs, args):
    spec = {
        "t": pl.BlockSpec((tokens, HEAD), lambda h: (0, h)),
        "s": pl.BlockSpec((pad, HEAD), lambda h: (h, 0)),
        "r": pl.BlockSpec((HEAD, tokens), lambda h: (h, 0)),
    }
    shape = {"t": (tokens, heads * HEAD), "s": (heads * pad, HEAD), "r": (heads * HEAD, tokens)}
    return pl.pallas_call(
        kernel,
        grid=(heads,),
        in_specs=[spec[i] for i in ins],
        out_specs=[spec[o] for o, _ in outs],
        out_shape=[jax.ShapeDtypeStruct(shape[o], d) for o, d in outs],
        compiler_params=pltpu.CompilerParams(vmem_limit_bytes=32 << 20),
        cost_estimate=pl.CostEstimate(
            flops=heads * 8 * tokens * tokens * HEAD, bytes_accessed=8 * tokens * heads * HEAD, transcendentals=0),
    )(*args)


def body(queries, keys, values, out_weight, out_grad):
    n = lax.axis_size("seq")
    tokens, width = queries.shape
    heads = width // HEAD
    pad = HEAD + 8
    while (heads * pad) % (8 * n):
        pad += 8
    run = functools.partial(per_head, heads=heads, tokens=tokens, pad=pad)
    plane = min(8, n)
    blocks = [list(range(at, at + plane)) for at in range(0, n, plane)]
    gathered = lax.all_gather(out_grad.astype(F32), "seq", axis_index_groups=blocks, tiled=True)
    (part,) = run(sum_kernel, ins="tt", outs=[("s", F32)], args=(keys, values))
    layers, low, levels = n // plane, bits_of(plane), bits_of(n)
    like = jax.ShapeDtypeStruct
    state, acts = part.shape, queries.shape
    mine, out_width = width // n, out_grad.shape[1]
    entry, attended_grad = remote_call(
        functools.partial(scan_kernel, n), 1, [like(state, F32), like(acts, F32)], [VM] * 3,
        scan_scratch(n, state), 32, (part, out_grad, out_weight))
    turned, part_grad = run(
        attend_kernel, ins="tttst", outs=[("r", F32), ("s", F32)],
        args=(queries, keys, values, entry, attended_grad))
    swap = (plane, layers, mine, tokens)
    rt, near, e_part, query_grad, key_part, value_part = remote_call(
        functools.partial(swap_kernel, n, plane), 2,
        [like(swap, F32), like(state, F32), like((state[0] >> low, HEAD), F32),
         like(acts, BF), like(acts, F32), like(acts, F32)],
        [VM] * 7,
        [pltpu.VMEM(state, F32)] * 3 + [DMA((levels,))] * 4 + [pltpu.VMEM(state, F32)] + [DMA((plane,))] * 2, 40,
        (part_grad, turned.reshape(layers, plane, mine, tokens), queries, keys, values, entry, attended_grad))
    tiles = 4
    key_grad, value_grad, weight_grad = remote_call(
        functools.partial(sum_out_kernel, n, plane), 3,
        [like(acts, BF), like(acts, BF), like((mine, out_width), F32)],
        [VM, pl.BlockSpec(memory_space=pl.ANY)] + [VM] * 6,
        [pltpu.VMEM(state, F32)] + [DMA((low,))] * 2 + [pltpu.VMEM(state, F32), pltpu.VMEM(gathered.shape, F32)]
        + [pltpu.VMEM((layers, mine, out_width), F32)] * 2
        + [DMA((tiles,))] + [DMA((tiles, layers))] * 2, 46,
        (rt, gathered, near, e_part, keys, values, key_part, value_part))
    return (query_grad, key_grad, value_grad, weight_grad)


def solution(mesh):
    rows = P(("groups", "seq"), None)
    return jax.shard_map(
        body, mesh=mesh, in_specs=(rows, rows, rows, P(), rows),
        out_specs=(rows, rows, rows, rows), check_vma=False)
```

```python
import functools

import jax
import jax.numpy as jnp
from jax import lax
from jax.experimental import pallas as pl
from jax.experimental.pallas import tpu as pltpu
from jax.sharding import PartitionSpec as P

HEAD = 128
MESH = pl.DeviceIdType.MESH
BF = jnp.bfloat16
F32 = jnp.float32
NN = (((1,), (0,)), ((), ()))
NT = (((1,), (1,)), ((), ()))
TN = (((0,), (0,)), ((), ()))


def split(x):
    if isinstance(x, tuple):
        return x
    if x.dtype == BF:
        return (x,)
    high = x.astype(BF)
    return (high, (x - high.astype(F32)).astype(BF))


def mm(a, b, dims):
    a, b = split(a), split(b)
    total = lax.dot_general(a[0], b[0], dims, preferred_element_type=F32)
    if len(a) > 1:
        total += lax.dot_general(a[1], b[0], dims, preferred_element_type=F32)
    if len(b) > 1:
        total += lax.dot_general(a[0], b[1], dims, preferred_element_type=F32)
    return total


def bits_of(n):
    count = n.bit_length() - 1
    assert 1 << count == n
    return count


def partner_of(me, k):
    return me + (1 - 2 * ((me // (1 << k)) % 2)) * (1 << k)


def sweep_up(n, reverse, x_ref, tot, recv, near, su, ru, work):
    me = lax.axis_index("seq")
    rows = x_ref.shape[0]
    base = 0
    levels = bits_of(n)
    for k in range(levels):
        half = rows >> (k + 1)
        off = rows - (rows >> k)
        bit = (me // (1 << k)) % 2
        keep = pl.multiple_of(base + bit * half, 8)
        give = pl.multiple_of(base + (1 - bit) * half, 8)
        src = x_ref if k == 0 else tot
        copy = pltpu.make_async_remote_copy(
            src_ref=src.at[pl.ds(give, half)], dst_ref=recv.at[pl.ds(off, half)],
            send_sem=su.at[k], recv_sem=ru.at[k],
            device_id={"seq": partner_of(me, k)}, device_id_type=MESH)
        copy.start()
        work()
        copy.wait()
        mine = src[pl.ds(keep, half), :]
        theirs = recv[pl.ds(off, half), :]
        near[pl.ds(off, half), :] = jnp.where(bit == (1 if reverse else 0), mine, theirs)
        if k + 1 < levels:
            tot[pl.ds(keep, half), :] = mine + theirs
        base = keep


def keeps_of(n, rows):
    me = lax.axis_index("seq")
    base, keeps = 0, []
    for k in range(bits_of(n)):
        half = rows >> (k + 1)
        bit = (me // (1 << k)) % 2
        base = pl.multiple_of(base + bit * half, 8)
        keeps.append((base, half, rows - (rows >> k), bit))
    return keeps


def sweep_down(keeps, bits, reverse, e_ref, near, out, sd, rd, work):
    me = lax.axis_index("seq")
    if len(keeps) - 1 in bits:
        keep, half, _, _ = keeps[-1]
        e_ref[pl.ds(keep, half), :] = jnp.zeros((half, e_ref.shape[1]), F32)
    for k in reversed(bits):
        keep, half, off, bit = keeps[k]
        early = bit == (1 if reverse else 0)
        now = e_ref[pl.ds(keep, half), :]
        past = now + near[pl.ds(off, half), :]
        out[pl.ds(off, half), :] = jnp.where(early, past, now)
        copy = pltpu.make_async_remote_copy(
            src_ref=out.at[pl.ds(off, half)], dst_ref=e_ref.at[pl.ds(keep, half)],
            send_sem=sd.at[k], recv_sem=rd.at[k],
            device_id={"seq": partner_of(me, k)}, device_id_type=MESH)
        copy.start()
        e_ref[pl.ds(keep, half), :] = jnp.where(early, now, past)
        work()
        copy.wait()


def greet(peers):
    barrier = pltpu.get_barrier_semaphore()
    for peer in peers:
        pl.semaphore_signal(barrier, inc=1, device_id={"seq": peer}, device_id_type=MESH)
    pl.semaphore_wait(barrier, len(peers))


def shares(heads, parts, one):
    left = iter(range(parts))

    def work():
        i = next(left)
        lax.fori_loop(heads * i // parts, heads * (i + 1) // parts, one, 0)

    return work


def scan_kernel(n, x_ref, og_ref, w_ref, e_ref, da_ref, tot, recv, near, out, su, ru, sd, rd):
    levels = bits_of(n)
    me = lax.axis_index("seq")

    def head(h, carry):
        at = pl.ds(pl.multiple_of(h * HEAD, HEAD), HEAD)
        da_ref[:, at] = lax.dot_general(og_ref[...], w_ref[at, :], NT, preferred_element_type=F32)
        return carry

    work = shares(w_ref.shape[0] // HEAD, 2 * levels, head)
    greet([partner_of(me, k) for k in range(levels)])
    sweep_up(n, False, x_ref, tot, recv, near, su, ru, work)
    sweep_down(keeps_of(n, x_ref.shape[0]), range(levels), False, e_ref, near, out, sd, rd, work)


def scan_scratch(n, shape):
    return [pltpu.VMEM(shape, F32)] * 4 + [pltpu.SemaphoreType.DMA((bits_of(n),))] * 4


VM = pl.BlockSpec(memory_space=pltpu.VMEM)
DMA = pltpu.SemaphoreType.DMA


def remote_call(kernel, collective_id, outs, ins, scratch, limit, args):
    return pl.pallas_call(
        kernel, out_shape=outs, in_specs=ins, out_specs=[VM] * len(outs), scratch_shapes=scratch,
        compiler_params=pltpu.CompilerParams(
            collective_id=collective_id, has_side_effects=True, vmem_limit_bytes=limit << 20),
        cost_estimate=pl.CostEstimate(flops=0, bytes_accessed=100_000_000, transcendentals=0),
    )(*args)


def swap_kernel(n, plane, x_ref, r_ref, q_ref, k_ref, v_ref, en_ref, da_ref,
                rt_ref, near, e_part, dq_ref, dk_ref, dv_ref, tot, recv, out, su, ru, sd, rd, e_ref, sp, rp):
    me = lax.axis_index("seq")
    layers = n // plane
    levels, low = bits_of(n), bits_of(plane)
    spot, layer = me % plane, me // plane
    near_peers = [layer * plane + (spot + j) % plane for j in range(1, plane)]
    far_peers = [partner_of(me, k) for k in range(low, levels)]
    greet(near_peers + far_peers)
    swaps = []
    for j in range(1, plane):
        swaps.append(pltpu.make_async_remote_copy(
            src_ref=r_ref.at[:, (spot + j) % plane], dst_ref=rt_ref.at[j],
            send_sem=sp.at[j], recv_sem=rp.at[j],
            device_id={"seq": near_peers[j - 1]}, device_id_type=MESH))
    heads = q_ref.shape[1] // HEAD
    pad = x_ref.shape[0] // heads

    def head(h, carry):
        cols = pl.ds(pl.multiple_of(h * HEAD, HEAD), HEAD)
        block = pl.ds(pl.multiple_of(h * pad, 8), pad)
        dq_ref[:, cols], dk_ref[:, cols], dv_ref[:, cols] = local_of(
            q_ref[:, cols], k_ref[:, cols], v_ref[:, cols], en_ref[block, :], da_ref[:, cols])
        return carry

    turns = iter(range(2 * levels))
    share = shares(heads, 2 * levels - low, head)

    def work():
        if next(turns) == low:
            for copy in swaps:
                copy.start()
        share()

    sweep_up(n, True, x_ref, tot, recv, near, su, ru, work)
    keeps = keeps_of(n, x_ref.shape[0])
    sweep_down(keeps, range(low, levels), True, e_ref, near, out, sd, rd, work)
    e_part[...] = e_ref[pl.ds(keeps[low - 1][0], e_part.shape[0]), :]
    rt_ref[0] = r_ref[:, spot]
    for copy in swaps:
        copy.wait()


def sum_out_kernel(n, plane, rt, og_ref, near, e_part, k_ref, v_ref, dkl_ref, dvl_ref,
                   dk_ref, dv_ref, w_ref, out, sd, rd, e_ref, og, part, zr, so, sz, rz):
    me = lax.axis_index("seq")
    layers = n // plane
    low = bits_of(plane)
    spot, layer = me % plane, me // plane
    tokens = rt.shape[3]
    tiles = so.shape[0]
    step = og.shape[1] // tiles
    loads = []
    for c in range(tiles):
        at = pl.ds(c * step, step)
        load = pltpu.make_async_copy(og_ref.at[:, at], og.at[:, at], so.at[c])
        load.start()
        loads.append(load)
    keeps = keeps_of(n, near.shape[0])
    e_ref[pl.ds(keeps[low - 1][0], e_part.shape[0]), :] = e_part[...]
    far_peers = [((layer + j) % layers) * plane + spot for j in range(1, layers)]
    greet(far_peers + [partner_of(me, k) for k in range(low)])
    sums = []
    for c in range(tiles):
        cols = pl.ds(c * step, step)
        loads[c].wait()
        acc = None
        for j in range(plane):
            rows = pl.ds(pl.multiple_of(((spot - j + plane) % plane) * tokens, tokens), tokens)
            left = rt[j].reshape(layers * rt.shape[2], tokens).astype(BF)
            term = lax.dot_general(left, og[rows, cols].astype(BF), NN, preferred_element_type=F32)
            acc = term if acc is None else acc + term
        part[:, :, cols] = acc.reshape(layers, rt.shape[2], step)
        for j in range(1, layers):
            copy = pltpu.make_async_remote_copy(
                src_ref=part.at[(layer + j) % layers, :, cols], dst_ref=zr.at[j, :, cols],
                send_sem=sz.at[c, j], recv_sem=rz.at[c, j],
                device_id={"seq": far_peers[j - 1]}, device_id_type=MESH)
            copy.start()
            sums.append(copy)
    sweep_down(keeps, range(low), True, e_ref, near, out, sd, rd, lambda: None)
    heads = k_ref.shape[1] // HEAD
    pad = near.shape[0] // heads

    def head(h, carry):
        cols = pl.ds(pl.multiple_of(h * HEAD, HEAD), HEAD)
        block = pl.ds(pl.multiple_of(h * pad, 8), pad)
        later = e_ref[block, :]
        fk, kslope = features(k_ref[:, cols])
        g = split(later[:HEAD, :])
        dfk = dkl_ref[:, cols] + mm(v_ref[:, cols], g, NN) + later[HEAD:HEAD + 1, :]
        dk_ref[:, cols] = (dfk * kslope).astype(BF)
        dv_ref[:, cols] = (dvl_ref[:, cols] + mm(fk, g, NT)).astype(BF)
        return carry

    lax.fori_loop(0, heads, head, 0)
    for copy in sums:
        copy.wait()
    total = part[layer]
    for j in range(1, layers):
        total = total + zr[j]
    w_ref[...] = total


def features(x):
    x = x.astype(F32)
    low = jnp.exp(jnp.minimum(x, 0.0))
    return jnp.where(x > 0, x + 1.0, low), low


def with_row(block, row, pad):
    row = jnp.where(lax.broadcasted_iota(jnp.int32, (pad - HEAD, HEAD), 0) == 0, row, 0.0)
    return jnp.concatenate([block, row], axis=0)


def sum_kernel(k_ref, v_ref, x_ref):
    fk, _ = features(k_ref[...])
    x_ref[...] = with_row(mm(v_ref[...], fk, TN), jnp.sum(fk, axis=0, keepdims=True), x_ref.shape[0])


def forward_of(q, k, v, entry):
    fq, qslope = features(q)
    fk, kslope = features(k)
    t = fq.shape[0]
    causal = lax.broadcasted_iota(jnp.int32, (t, t), 1) <= lax.broadcasted_iota(jnp.int32, (t, t), 0)
    fq_s, fk_s = split(fq), split(fk)
    scores = jnp.where(causal, mm(fq_s, fk_s, NT), 0.0)
    z = entry[HEAD:HEAD + 1, :]
    den = jnp.sum(scores, axis=1, keepdims=True) + jnp.sum(fq * z, axis=1, keepdims=True)
    scores = split(scores)
    numer = mm(scores, v, NN) + mm(fq_s, entry[:HEAD, :], NT)
    inv = 1.0 / den
    return fq, fq_s, qslope, fk_s, causal, scores, z, inv, numer * inv


def attend_kernel(q_ref, k_ref, v_ref, e_ref, da_ref, r_ref, g_ref):
    fq, fq_s, _, _, _, _, _, inv, att = forward_of(q_ref[...], k_ref[...], v_ref[...], e_ref[...])
    r_ref[...] = att.T
    dn = da_ref[...] * inv
    dden = -jnp.sum(dn * att, axis=1, keepdims=True)
    g_ref[...] = with_row(mm(dn, fq_s, TN), jnp.sum(fq * dden, axis=0, keepdims=True), g_ref.shape[0])


def local_of(q, k, v, entry, da):
    fq, fq_s, qslope, fk_s, causal, scores, z, inv, att = forward_of(q, k, v, entry)
    dn = da * inv
    dden = -jnp.sum(dn * att, axis=1, keepdims=True)
    dn_s = split(dn)
    dp = split(jnp.where(causal, mm(dn_s, v, NT) + dden, 0.0))
    dfq = mm(dp, fk_s, NN) + mm(dn_s, entry[:HEAD, :], NN) + dden * z
    return (dfq * qslope).astype(BF), mm(dp, fq_s, TN), mm(scores, dn_s, TN)


def per_head(kernel, heads, tokens, pad, ins, outs, args):
    spec = {
        "t": pl.BlockSpec((tokens, HEAD), lambda h: (0, h)),
        "s": pl.BlockSpec((pad, HEAD), lambda h: (h, 0)),
        "r": pl.BlockSpec((HEAD, tokens), lambda h: (h, 0)),
    }
    shape = {"t": (tokens, heads * HEAD), "s": (heads * pad, HEAD), "r": (heads * HEAD, tokens)}
    return pl.pallas_call(
        kernel,
        grid=(heads,),
        in_specs=[spec[i] for i in ins],
        out_specs=[spec[o] for o, _ in outs],
        out_shape=[jax.ShapeDtypeStruct(shape[o], d) for o, d in outs],
        compiler_params=pltpu.CompilerParams(vmem_limit_bytes=32 << 20),
        cost_estimate=pl.CostEstimate(
            flops=heads * 8 * tokens * tokens * HEAD, bytes_accessed=8 * tokens * heads * HEAD, transcendentals=0),
    )(*args)


def body(queries, keys, values, out_weight, out_grad):
    n = lax.axis_size("seq")
    tokens, width = queries.shape
    heads = width // HEAD
    pad = HEAD + 8
    while (heads * pad) % (8 * n):
        pad += 8
    run = functools.partial(per_head, heads=heads, tokens=tokens, pad=pad)
    plane = min(8, n)
    blocks = [list(range(at, at + plane)) for at in range(0, n, plane)]
    gathered = lax.all_gather(out_grad.astype(F32), "seq", axis_index_groups=blocks, tiled=True)
    (part,) = run(sum_kernel, ins="tt", outs=[("s", F32)], args=(keys, values))
    layers, low, levels = n // plane, bits_of(plane), bits_of(n)
    like = jax.ShapeDtypeStruct
    state, acts = part.shape, queries.shape
    mine, out_width = width // n, out_grad.shape[1]
    entry, attended_grad = remote_call(
        functools.partial(scan_kernel, n), 1, [like(state, F32), like(acts, F32)], [VM] * 3,
        scan_scratch(n, state), 12, (part, out_grad, out_weight))
    turned, part_grad = run(
        attend_kernel, ins="tttst", outs=[("r", F32), ("s", F32)],
        args=(queries, keys, values, entry, attended_grad))
    swap = (plane, layers, mine, tokens)
    rt, near, e_part, query_grad, key_part, value_part = remote_call(
        functools.partial(swap_kernel, n, plane), 2,
        [like(swap, F32), like(state, F32), like((state[0] >> low, HEAD), F32),
         like(acts, BF), like(acts, F32), like(acts, F32)],
        [VM] * 7,
        [pltpu.VMEM(state, F32)] * 3 + [DMA((levels,))] * 4 + [pltpu.VMEM(state, F32)] + [DMA((plane,))] * 2, 12,
        (part_grad, turned.reshape(layers, plane, mine, tokens), queries, keys, values, entry, attended_grad))
    tiles = 4
    key_grad, value_grad, weight_grad = remote_call(
        functools.partial(sum_out_kernel, n, plane), 3,
        [like(acts, BF), like(acts, BF), like((mine, out_width), F32)],
        [VM, pl.BlockSpec(memory_space=pl.ANY)] + [VM] * 6,
        [pltpu.VMEM(state, F32)] + [DMA((low,))] * 2 + [pltpu.VMEM(state, F32), pltpu.VMEM(gathered.shape, F32)]
        + [pltpu.VMEM((layers, mine, out_width), F32)] * 2
        + [DMA((tiles,))] + [DMA((tiles, layers))] * 2, 28,
        (rt, gathered, near, e_part, keys, values, key_part, value_part))
    return (query_grad, key_grad, value_grad, weight_grad)


def solution(mesh):
    rows = P(("groups", "seq"), None)
    return jax.shard_map(
        body, mesh=mesh, in_specs=(rows, rows, rows, P(), rows),
        out_specs=(rows, rows, rows, rows), check_vma=False)
```

```python
import functools

import jax
import jax.numpy as jnp
from jax import lax
from jax.experimental import pallas as pl
from jax.experimental.pallas import tpu as pltpu
from jax.sharding import PartitionSpec as P

HEAD = 128
MESH = pl.DeviceIdType.MESH
BF = jnp.bfloat16
F32 = jnp.float32
NN = (((1,), (0,)), ((), ()))
NT = (((1,), (1,)), ((), ()))
TN = (((0,), (0,)), ((), ()))


def split(x):
    if isinstance(x, tuple):
        return x
    if x.dtype == BF:
        return (x,)
    high = x.astype(BF)
    return (high, (x - high.astype(F32)).astype(BF))


def mm(a, b, dims):
    a, b = split(a), split(b)
    total = lax.dot_general(a[0], b[0], dims, preferred_element_type=F32)
    if len(a) > 1:
        total += lax.dot_general(a[1], b[0], dims, preferred_element_type=F32)
    if len(b) > 1:
        total += lax.dot_general(a[0], b[1], dims, preferred_element_type=F32)
    return total


def bits_of(n):
    count = n.bit_length() - 1
    assert 1 << count == n
    return count


def partner_of(me, k):
    return me + (1 - 2 * ((me // (1 << k)) % 2)) * (1 << k)


def sweep_up(n, reverse, x_ref, tot, recv, near, su, ru, work):
    me = lax.axis_index("seq")
    rows = x_ref.shape[0]
    base = 0
    levels = bits_of(n)
    for k in range(levels):
        half = rows >> (k + 1)
        off = rows - (rows >> k)
        bit = (me // (1 << k)) % 2
        keep = pl.multiple_of(base + bit * half, 8)
        give = pl.multiple_of(base + (1 - bit) * half, 8)
        src = x_ref if k == 0 else tot
        copy = pltpu.make_async_remote_copy(
            src_ref=src.at[pl.ds(give, half)], dst_ref=recv.at[pl.ds(off, half)],
            send_sem=su.at[k], recv_sem=ru.at[k],
            device_id={"seq": partner_of(me, k)}, device_id_type=MESH)
        copy.start()
        work()
        copy.wait()
        mine = src[pl.ds(keep, half), :]
        theirs = recv[pl.ds(off, half), :]
        near[pl.ds(off, half), :] = jnp.where(bit == (1 if reverse else 0), mine, theirs)
        if k + 1 < levels:
            tot[pl.ds(keep, half), :] = mine + theirs
        base = keep


def keeps_of(n, rows):
    me = lax.axis_index("seq")
    base, keeps = 0, []
    for k in range(bits_of(n)):
        half = rows >> (k + 1)
        bit = (me // (1 << k)) % 2
        base = pl.multiple_of(base + bit * half, 8)
        keeps.append((base, half, rows - (rows >> k), bit))
    return keeps


def sweep_down(keeps, bits, reverse, e_ref, near, out, sd, rd, work):
    me = lax.axis_index("seq")
    if len(keeps) - 1 in bits:
        keep, half, _, _ = keeps[-1]
        e_ref[pl.ds(keep, half), :] = jnp.zeros((half, e_ref.shape[1]), F32)
    for k in reversed(bits):
        keep, half, off, bit = keeps[k]
        early = bit == (1 if reverse else 0)
        now = e_ref[pl.ds(keep, half), :]
        past = now + near[pl.ds(off, half), :]
        out[pl.ds(off, half), :] = jnp.where(early, past, now)
        copy = pltpu.make_async_remote_copy(
            src_ref=out.at[pl.ds(off, half)], dst_ref=e_ref.at[pl.ds(keep, half)],
            send_sem=sd.at[k], recv_sem=rd.at[k],
            device_id={"seq": partner_of(me, k)}, device_id_type=MESH)
        copy.start()
        e_ref[pl.ds(keep, half), :] = jnp.where(early, now, past)
        work()
        copy.wait()


def greet(peers):
    barrier = pltpu.get_barrier_semaphore()
    for peer in peers:
        pl.semaphore_signal(barrier, inc=1, device_id={"seq": peer}, device_id_type=MESH)
    pl.semaphore_wait(barrier, len(peers))


def shares(heads, parts, one):
    left = iter(range(parts))

    def work():
        i = next(left)
        lax.fori_loop(heads * i // parts, heads * (i + 1) // parts, one, 0)

    return work


def scan_kernel(n, x_ref, og_ref, w_ref, e_ref, da_ref, tot, recv, near, out, su, ru, sd, rd):
    levels = bits_of(n)
    me = lax.axis_index("seq")

    def head(h, carry):
        at = pl.ds(pl.multiple_of(h * HEAD, HEAD), HEAD)
        da_ref[:, at] = lax.dot_general(og_ref[...], w_ref[at, :], NT, preferred_element_type=F32)
        return carry

    work = shares(w_ref.shape[0] // HEAD, 2 * levels, head)
    greet([partner_of(me, k) for k in range(levels)])
    sweep_up(n, False, x_ref, tot, recv, near, su, ru, work)
    sweep_down(keeps_of(n, x_ref.shape[0]), range(levels), False, e_ref, near, out, sd, rd, work)


def scan_scratch(n, shape):
    return [pltpu.VMEM(shape, F32)] * 4 + [pltpu.SemaphoreType.DMA((bits_of(n),))] * 4


VM = pl.BlockSpec(memory_space=pltpu.VMEM)
DMA = pltpu.SemaphoreType.DMA


def remote_call(kernel, collective_id, outs, ins, scratch, limit, args):
    return pl.pallas_call(
        kernel, out_shape=outs, in_specs=ins, out_specs=[VM] * len(outs), scratch_shapes=scratch,
        compiler_params=pltpu.CompilerParams(
            collective_id=collective_id, has_side_effects=True, vmem_limit_bytes=limit << 20),
        cost_estimate=pl.CostEstimate(flops=0, bytes_accessed=100_000_000, transcendentals=0),
    )(*args)


def swap_kernel(n, plane, x_ref, r_ref, q_ref, k_ref, v_ref, en_ref, da_ref,
                rt_ref, near, e_part, dq_ref, dk_ref, dv_ref, tot, recv, out, su, ru, sd, rd, e_ref, sp, rp):
    me = lax.axis_index("seq")
    layers = n // plane
    levels, low = bits_of(n), bits_of(plane)
    spot, layer = me % plane, me // plane
    near_peers = [layer * plane + (spot + j) % plane for j in range(1, plane)]
    far_peers = [partner_of(me, k) for k in range(low, levels)]
    greet(near_peers + far_peers)
    swaps = []
    for j in range(1, plane):
        swaps.append(pltpu.make_async_remote_copy(
            src_ref=r_ref.at[:, (spot + j) % plane], dst_ref=rt_ref.at[j],
            send_sem=sp.at[j], recv_sem=rp.at[j],
            device_id={"seq": near_peers[j - 1]}, device_id_type=MESH))
    heads = q_ref.shape[1] // HEAD
    pad = x_ref.shape[0] // heads

    def head(h, carry):
        cols = pl.ds(pl.multiple_of(h * HEAD, HEAD), HEAD)
        block = pl.ds(pl.multiple_of(h * pad, 8), pad)
        dq_ref[:, cols], dk_ref[:, cols], dv_ref[:, cols] = local_of(
            q_ref[:, cols], k_ref[:, cols], v_ref[:, cols], en_ref[block, :], da_ref[:, cols])
        return carry

    turns = iter(range(2 * levels))
    share = shares(heads, 2 * levels - low, head)

    def work():
        if next(turns) == low - 1:
            for copy in swaps:
                copy.start()
        share()

    sweep_up(n, True, x_ref, tot, recv, near, su, ru, work)
    keeps = keeps_of(n, x_ref.shape[0])
    sweep_down(keeps, range(low, levels), True, e_ref, near, out, sd, rd, work)
    e_part[...] = e_ref[pl.ds(keeps[low - 1][0], e_part.shape[0]), :]
    rt_ref[0] = r_ref[:, spot]
    for copy in swaps:
        copy.wait()


def sum_out_kernel(n, plane, rt, og_ref, near, e_part, k_ref, v_ref, dkl_ref, dvl_ref,
                   dk_ref, dv_ref, w_ref, out, sd, rd, e_ref, og, part, zr, so, sz, rz):
    me = lax.axis_index("seq")
    layers = n // plane
    low = bits_of(plane)
    spot, layer = me % plane, me // plane
    tokens = rt.shape[3]
    tiles = so.shape[0]
    step = og.shape[1] // tiles
    loads = []
    for c in range(tiles):
        at = pl.ds(c * step, step)
        load = pltpu.make_async_copy(og_ref.at[:, at], og.at[:, at], so.at[c])
        load.start()
        loads.append(load)
    keeps = keeps_of(n, near.shape[0])
    e_ref[pl.ds(keeps[low - 1][0], e_part.shape[0]), :] = e_part[...]
    far_peers = [((layer + j) % layers) * plane + spot for j in range(1, layers)]
    greet(far_peers + [partner_of(me, k) for k in range(low)])
    sums = []
    for c in range(tiles):
        cols = pl.ds(c * step, step)
        loads[c].wait()
        acc = None
        for j in range(plane):
            rows = pl.ds(pl.multiple_of(((spot - j + plane) % plane) * tokens, tokens), tokens)
            left = rt[j].reshape(layers * rt.shape[2], tokens).astype(BF)
            term = lax.dot_general(left, og[rows, cols].astype(BF), NN, preferred_element_type=F32)
            acc = term if acc is None else acc + term
        part[:, :, cols] = acc.reshape(layers, rt.shape[2], step)
        for j in range(1, layers):
            copy = pltpu.make_async_remote_copy(
                src_ref=part.at[(layer + j) % layers, :, cols], dst_ref=zr.at[j, :, cols],
                send_sem=sz.at[c, j], recv_sem=rz.at[c, j],
                device_id={"seq": far_peers[j - 1]}, device_id_type=MESH)
            copy.start()
            sums.append(copy)
    sweep_down(keeps, range(low), True, e_ref, near, out, sd, rd, lambda: None)
    heads = k_ref.shape[1] // HEAD
    pad = near.shape[0] // heads

    def head(h, carry):
        cols = pl.ds(pl.multiple_of(h * HEAD, HEAD), HEAD)
        block = pl.ds(pl.multiple_of(h * pad, 8), pad)
        later = e_ref[block, :]
        fk, kslope = features(k_ref[:, cols])
        g = split(later[:HEAD, :])
        dfk = dkl_ref[:, cols] + mm(v_ref[:, cols], g, NN) + later[HEAD:HEAD + 1, :]
        dk_ref[:, cols] = (dfk * kslope).astype(BF)
        dv_ref[:, cols] = (dvl_ref[:, cols] + mm(fk, g, NT)).astype(BF)
        return carry

    lax.fori_loop(0, heads, head, 0)
    for copy in sums:
        copy.wait()
    total = part[layer]
    for j in range(1, layers):
        total = total + zr[j]
    w_ref[...] = total


def features(x):
    x = x.astype(F32)
    low = jnp.exp(jnp.minimum(x, 0.0))
    return jnp.where(x > 0, x + 1.0, low), low


def with_row(block, row, pad):
    row = jnp.where(lax.broadcasted_iota(jnp.int32, (pad - HEAD, HEAD), 0) == 0, row, 0.0)
    return jnp.concatenate([block, row], axis=0)


def sum_kernel(k_ref, v_ref, x_ref):
    fk, _ = features(k_ref[...])
    x_ref[...] = with_row(mm(v_ref[...], fk, TN), jnp.sum(fk, axis=0, keepdims=True), x_ref.shape[0])


def forward_of(q, k, v, entry):
    fq, qslope = features(q)
    fk, kslope = features(k)
    t = fq.shape[0]
    causal = lax.broadcasted_iota(jnp.int32, (t, t), 1) <= lax.broadcasted_iota(jnp.int32, (t, t), 0)
    fq_s, fk_s = split(fq), split(fk)
    scores = jnp.where(causal, mm(fq_s, fk_s, NT), 0.0)
    z = entry[HEAD:HEAD + 1, :]
    den = jnp.sum(scores, axis=1, keepdims=True) + jnp.sum(fq * z, axis=1, keepdims=True)
    scores = split(scores)
    numer = mm(scores, v, NN) + mm(fq_s, entry[:HEAD, :], NT)
    inv = 1.0 / den
    return fq, fq_s, qslope, fk_s, causal, scores, z, inv, numer * inv


def attend_kernel(q_ref, k_ref, v_ref, e_ref, da_ref, r_ref, g_ref):
    fq, fq_s, _, _, _, _, _, inv, att = forward_of(q_ref[...], k_ref[...], v_ref[...], e_ref[...])
    r_ref[...] = att.T
    dn = da_ref[...] * inv
    dden = -jnp.sum(dn * att, axis=1, keepdims=True)
    g_ref[...] = with_row(mm(dn, fq_s, TN), jnp.sum(fq * dden, axis=0, keepdims=True), g_ref.shape[0])


def local_of(q, k, v, entry, da):
    fq, fq_s, qslope, fk_s, causal, scores, z, inv, att = forward_of(q, k, v, entry)
    dn = da * inv
    dden = -jnp.sum(dn * att, axis=1, keepdims=True)
    dn_s = split(dn)
    dp = split(jnp.where(causal, mm(dn_s, v, NT) + dden, 0.0))
    dfq = mm(dp, fk_s, NN) + mm(dn_s, entry[:HEAD, :], NN) + dden * z
    return (dfq * qslope).astype(BF), mm(dp, fq_s, TN), mm(scores, dn_s, TN)


def per_head(kernel, heads, tokens, pad, ins, outs, args):
    spec = {
        "t": pl.BlockSpec((tokens, HEAD), lambda h: (0, h)),
        "s": pl.BlockSpec((pad, HEAD), lambda h: (h, 0)),
        "r": pl.BlockSpec((HEAD, tokens), lambda h: (h, 0)),
    }
    shape = {"t": (tokens, heads * HEAD), "s": (heads * pad, HEAD), "r": (heads * HEAD, tokens)}
    return pl.pallas_call(
        kernel,
        grid=(heads,),
        in_specs=[spec[i] for i in ins],
        out_specs=[spec[o] for o, _ in outs],
        out_shape=[jax.ShapeDtypeStruct(shape[o], d) for o, d in outs],
        compiler_params=pltpu.CompilerParams(vmem_limit_bytes=32 << 20),
        cost_estimate=pl.CostEstimate(
            flops=heads * 8 * tokens * tokens * HEAD, bytes_accessed=8 * tokens * heads * HEAD, transcendentals=0),
    )(*args)


def body(queries, keys, values, out_weight, out_grad):
    n = lax.axis_size("seq")
    tokens, width = queries.shape
    heads = width // HEAD
    pad = HEAD + 8
    while (heads * pad) % (8 * n):
        pad += 8
    run = functools.partial(per_head, heads=heads, tokens=tokens, pad=pad)
    plane = min(8, n)
    blocks = [list(range(at, at + plane)) for at in range(0, n, plane)]
    gathered = lax.all_gather(out_grad.astype(F32), "seq", axis_index_groups=blocks, tiled=True)
    (part,) = run(sum_kernel, ins="tt", outs=[("s", F32)], args=(keys, values))
    layers, low, levels = n // plane, bits_of(plane), bits_of(n)
    like = jax.ShapeDtypeStruct
    state, acts = part.shape, queries.shape
    mine, out_width = width // n, out_grad.shape[1]
    entry, attended_grad = remote_call(
        functools.partial(scan_kernel, n), 1, [like(state, F32), like(acts, F32)], [VM] * 3,
        scan_scratch(n, state), 12, (part, out_grad, out_weight))
    turned, part_grad = run(
        attend_kernel, ins="tttst", outs=[("r", F32), ("s", F32)],
        args=(queries, keys, values, entry, attended_grad))
    swap = (plane, layers, mine, tokens)
    rt, near, e_part, query_grad, key_part, value_part = remote_call(
        functools.partial(swap_kernel, n, plane), 2,
        [like(swap, F32), like(state, F32), like((state[0] >> low, HEAD), F32),
         like(acts, BF), like(acts, F32), like(acts, F32)],
        [VM] * 7,
        [pltpu.VMEM(state, F32)] * 3 + [DMA((levels,))] * 4 + [pltpu.VMEM(state, F32)] + [DMA((plane,))] * 2, 12,
        (part_grad, turned.reshape(layers, plane, mine, tokens), queries, keys, values, entry, attended_grad))
    tiles = 4
    key_grad, value_grad, weight_grad = remote_call(
        functools.partial(sum_out_kernel, n, plane), 3,
        [like(acts, BF), like(acts, BF), like((mine, out_width), F32)],
        [VM, pl.BlockSpec(memory_space=pl.ANY)] + [VM] * 6,
        [pltpu.VMEM(state, F32)] + [DMA((low,))] * 2 + [pltpu.VMEM(state, F32), pltpu.VMEM(gathered.shape, F32)]
        + [pltpu.VMEM((layers, mine, out_width), F32)] * 2
        + [DMA((tiles,))] + [DMA((tiles, layers))] * 2, 28,
        (rt, gathered, near, e_part, keys, values, key_part, value_part))
    return (query_grad, key_grad, value_grad, weight_grad)


def solution(mesh):
    rows = P(("groups", "seq"), None)
    return jax.shard_map(
        body, mesh=mesh, in_specs=(rows, rows, rows, P(), rows),
        out_specs=(rows, rows, rows, rows), check_vma=False)
```
